256 devices in a mesh: px: 32 (over z, x), py: 8 (over y, core).
Axes of the slice: x: 4, y: 4, z: 8, core: 2. Of those that a mesh axis runs over, the one named last changes fastest.
Arguments:
- field: float32 [512, 512, 1024], P('px', 'py'), may hold values from -120 to 120
- seeds_first: int32 [512, 128], replicated, may hold values from -64 to 63
- seeds_second: int32 [512, 128], replicated, may hold values from -64 to 63
Outputs:
- basis_first: float32 [512, 128], replicated
- basis_second: float32 [512, 128], replicated
- core_tensor: float32 [128, 128, 1024], P('px', 'py')
The draws below stay inside these ranges and needn't reach their ends.
All inputs are finite; a program needn't handle non-finite values.
Results may differ from the reference program's by a relative error of at most 0.0003.
Values sent between devices are 32-bit elements; how exact they have to be, the bound alone decides.
No kernel may reach another device: no remote copies, remote signals or barrier semaphores. Data moves between devices by JAX's collectives and lax.ppermute only.
A program may use at most 128 MiB of HBM per device.

```python
import math
import jax
import jax.numpy as jnp
from jax import lax

N1 = 512
N2 = 512
RANK = 128
POINTS = 1024
ITERS = 4


def draw_field(key, part):
    key_base = jax.random.fold_in(key, 11)
    key_first = jax.random.fold_in(key, 12)
    key_second = jax.random.fold_in(key, 13)
    base_noise = jnp.clip(jax.random.normal(key_base, (N1, N2, POINTS), jnp.float32), -6.0, 6.0)
    mixed = base_noise + 0.6 * jnp.roll(base_noise, 1, 0) + 0.6 * jnp.roll(base_noise, 1, 1)
    scale_first = jnp.exp(jax.random.uniform(key_first, (N1,), jnp.float32, math.log(0.3), math.log(3.0)))
    scale_second = jnp.exp(jax.random.uniform(key_second, (N2,), jnp.float32, math.log(0.3), math.log(3.0)))
    return mixed * scale_first[:, None, None] * scale_second[None, :, None]


def plant(drawn, own_key, smallest, high):
    longest = drawn.shape.index(max(drawn.shape))
    spots = []
    for shift in (0, 1):
        where = [jax.random.randint(jax.random.fold_in(own_key, axis), (), 0, length) for axis, length in enumerate(drawn.shape)]
        where[longest] = (where[longest] + shift) % drawn.shape[longest]
        spots.append(tuple(where))
    return drawn.at[spots[0]].set(smallest).at[spots[1]].set(high)


def setup_inputs(seed: int = 0) -> dict:
    key_list = jax.random.split(jax.random.key(seed), 4)
    return {
        "field": draw_field(jax.random.fold_in(key_list[3], 71), 0),
        "seeds_first": plant(jax.random.randint(key_list[1], (N1, RANK), -64, 64), jax.random.fold_in(key_list[1], 1), -64, 63).astype(jnp.int32),
        "seeds_second": plant(jax.random.randint(key_list[2], (N2, RANK), -64, 64), jax.random.fold_in(key_list[2], 1), -64, 63).astype(jnp.int32),
    }


def orthonormal(matrix):
    inner = jnp.dot(matrix.T, matrix, precision=lax.Precision.HIGHEST)
    factor = jnp.linalg.cholesky(inner)
    return jax.scipy.linalg.solve_triangular(factor, matrix.T, lower=True).T

def leading_basis(gram, seeds):
    basis = orthonormal(seeds.astype(jnp.float32))
    for sweep in range(ITERS):
        basis = orthonormal(jnp.dot(gram, basis, precision=lax.Precision.HIGHEST))
    return basis

def reference(field, seeds_first, seeds_second):
    flattened = field.reshape(N1, N2 * POINTS)
    gram_first = jnp.dot(flattened, flattened.T, precision=lax.Precision.HIGHEST)
    basis_first = leading_basis(gram_first, seeds_first)
    reduced = jnp.dot(basis_first.T, flattened, precision=lax.Precision.HIGHEST).reshape(RANK, N2, POINTS)
    turned = jnp.transpose(reduced, (1, 0, 2)).reshape(N2, RANK * POINTS)
    gram_second = jnp.dot(turned, turned.T, precision=lax.Precision.HIGHEST)
    basis_second = leading_basis(gram_second, seeds_second)
    core_tensor = jnp.einsum('jb,ajp->abp', basis_second, reduced, precision=lax.Precision.HIGHEST)
    return (basis_first, basis_second, core_tensor)
```

```python
import jax
import jax.numpy as jnp
from jax import lax
from jax.sharding import Mesh, PartitionSpec as P

ITERS = 4
HI = lax.Precision.HIGHEST


def orthonormal(matrix):
    inner = jnp.dot(matrix.T, matrix, precision=HI)
    factor = jnp.linalg.cholesky(inner)
    return jax.scipy.linalg.solve_triangular(factor, matrix.T, lower=True).T


def total_gram(partial):
    tiles = partial.reshape(64, 8, 4, 128).transpose(0, 2, 1, 3).reshape(8, 32, 8, 128)
    got = lax.all_to_all(tiles, ("y", "c"), 0, 0, tiled=True)
    mine = jnp.sum(got, axis=0)
    got = lax.all_to_all(mine, ("z", "x"), 0, 0, tiled=True)
    one = jnp.sum(got, axis=0, keepdims=True)
    row = lax.all_to_all(jnp.broadcast_to(one, (32, 8, 128)), ("z", "x"), 0, 0, tiled=True)
    whole = lax.all_to_all(
        jnp.broadcast_to(row[None], (8, 32, 8, 128)), ("y", "c"), 0, 0, tiled=True
    )
    return whole.reshape(64, 4, 8, 128).transpose(0, 2, 1, 3).reshape(512, 512)


def leading_basis(gram, basis):
    for sweep in range(ITERS):
        basis = orthonormal(jnp.dot(gram, basis, precision=HI))
    return basis


def local(field, seeds_first, seeds_second):
    sent = field.reshape(16, 4, 16, 8, 128).transpose(3, 1, 0, 2, 4).reshape(32, 16, 16, 128)
    fibers = lax.all_to_all(sent, ("z", "x"), 0, 0, tiled=True)
    start_first = orthonormal(seeds_first.astype(jnp.float32))
    start_second = orthonormal(seeds_second.astype(jnp.float32))
    flat = fibers.reshape(512, 2048)
    partial_first = jnp.dot(flat, flat.T, precision=HI)
    basis_first = leading_basis(total_gram(partial_first), start_first)
    reduced = jnp.dot(basis_first.T, flat, precision=HI)
    slab = lax.all_to_all(reduced.reshape(32, 4, 16, 128), ("y", "c", "x"), 0, 0, tiled=True)
    turned = slab.transpose(0, 2, 1, 3).reshape(512, 512)
    partial_second = jnp.dot(turned, turned.T, precision=HI)
    basis_second = leading_basis(total_gram(partial_second), start_second)
    core = jnp.dot(basis_second.T, turned, precision=HI).reshape(8, 16, 4, 128)
    core = lax.all_to_all(core, ("y", "c"), 0, 0, tiled=True)
    core = lax.all_to_all(core, "z", 0, 0, tiled=True)
    core = core.transpose(2, 1, 0, 3).reshape(4, 16, 1024)
    return (basis_first, basis_second, core)


def solution(mesh):
    fine = Mesh(mesh.devices.reshape(8, 4, 4, 2), ("z", "x", "y", "c"))
    return jax.shard_map(
        local,
        mesh=fine,
        in_specs=(P(("z", "x"), ("y", "c"), None), P(), P()),
        out_specs=(P(), P(), P(("z", "x"), ("y", "c"), None)),
        check_vma=False,
    )
```

```python
import jax
import jax.numpy as jnp
from jax import lax
from jax.experimental import pallas as pl
from jax.experimental.pallas import tpu as pltpu
from jax.sharding import Mesh, PartitionSpec as P

ITERS = 4
N = 512
RANK = 128
F32 = jnp.float32
BF16 = jnp.bfloat16
NN = (((1,), (0,)), ((), ()))
NT = (((1,), (1,)), ((), ()))
TILES = [(row, col) for row in range(64) for col in range(row // 16, 4)]
HALF = len(TILES) // 2
PARAMS = pltpu.CompilerParams(vmem_limit_bytes=56 * 2**20)
VMEM = pl.BlockSpec(memory_space=pltpu.VMEM)
SMEM = pl.BlockSpec(memory_space=pltpu.SMEM)
ANY = pl.BlockSpec(memory_space=pl.ANY)


def dot(left, right, dims):
    return lax.dot_general(left, right, dims, preferred_element_type=F32)


def split(x):
    high = x.astype(BF16)
    return high, (x - high.astype(F32)).astype(BF16)


def as_left(x):
    high, low = split(x)
    return jnp.concatenate([high, low, high], axis=1)


def as_right_rows(x):
    high, low = split(x)
    return jnp.concatenate([high, high, low], axis=0)


def as_right_cols(x):
    high, low = split(x)
    return jnp.concatenate([high, high, low], axis=1)


def inverse_factor(inner):
    sub = lax.broadcasted_iota(jnp.int32, (8, RANK), 0)
    lane = lax.broadcasted_iota(jnp.int32, (8, RANK), 1)
    panels = RANK // 8
    left = [inner[8 * i : 8 * i + 8, :] for i in range(panels)]
    right = [jnp.where(lane == sub + 8 * i, 1.0, 0.0).astype(F32) for i in range(panels)]
    spread = lambda row: jnp.broadcast_to(row, (8, RANK))
    out = []
    for p in range(panels):
        rows = range(p, panels)
        cols = {i: [spread(left[i][:, 8 * p + t : 8 * p + t + 1]) for t in range(8)] for i in rows}
        done = jnp.zeros((8, RANK), F32)
        for t in range(8):
            root = lax.rsqrt(spread(cols[p][t][t : t + 1, :]))
            left_row = spread(left[p][t : t + 1, :]) * root
            right_row = spread(right[p][t : t + 1, :]) * root
            done = jnp.where(sub == t, right_row, done)
            ahead = [spread(cols[p][u][t : t + 1, :]) * root for u in range(t + 1, 8)]
            for i in rows:
                factor = cols[i][t] * root
                left[i] = left[i] - factor * left_row
                right[i] = right[i] - factor * right_row
                for k, u in enumerate(range(t + 1, 8)):
                    cols[i][u] = cols[i][u] - factor * ahead[k]
        out.append(done)
    return jnp.concatenate(out, axis=0)


def orthonormal(turned):
    inner = dot(as_left(turned), as_right_cols(turned), NT)
    return dot(as_left(inverse_factor(inner)), as_right_rows(turned), NN)


def seeds_kernel(first_ref, second_ref, first_out, second_out):
    first_out[...] = orthonormal(first_ref[...].astype(F32))
    second_out[...] = orthonormal(second_ref[...].astype(F32))


def upper_gram(high, low, mine_ref, other_ref, swap, core):
    for block in range(4):
        rows = slice(128 * block, 128 * block + 128)
        cols = slice(128 * block, N)
        gram = dot(
            jnp.concatenate([high[rows, :], low[rows, :], high[rows, :]], axis=1),
            jnp.concatenate([high[cols, :], high[cols, :], low[cols, :]], axis=1),
            NT,
        )
        for at, (row, col) in enumerate(TILES):
            if row // 16 == block:
                r, c = 8 * (row % 16), 128 * (col - block)
                half = lax.bitwise_xor(at // HALF, core)
                swap[half, at % HALF] = gram[r : r + 8, c : c + 128]
    mine_ref[...] = swap[0]
    other_ref[...] = swap[1]


def first_gram_kernel(core_ref, fibers_ref, mine_ref, other_ref, high, low, swap):
    flat = fibers_ref.reshape(N * 16, 128)
    for j in range(16):
        h, l = split(flat[pl.ds(j, N, stride=16), :])
        high[:, 128 * j : 128 * j + 128] = h
        low[:, 128 * j : 128 * j + 128] = l
    upper_gram(high, low, mine_ref, other_ref, swap, core_ref[0])


def second_gram_kernel(core_ref, slab_ref, mine_ref, other_ref, high, low, swap):
    for a in range(4):
        h, l = split(slab_ref[:, a].reshape(N, 128))
        high[:, 128 * a : 128 * a + 128] = h
        low[:, 128 * a : 128 * a + 128] = l
    upper_gram(high, low, mine_ref, other_ref, swap, core_ref[0])


def leading(core_ref, mine_ref, other_ref, start_ref, whole, gram, parts):
    core = core_ref[0]
    whole[core] = mine_ref[...]
    whole[1 - core] = other_ref[...]
    for at, (row, col) in enumerate(TILES):
        gram[8 * row : 8 * row + 8, 128 * col : 128 * col + 128] = whole[at // HALF, at % HALF]
    for row in range(1, 4):
        for col in range(row):
            gram[128 * row : 128 * row + 128, 128 * col : 128 * col + 128] = gram[
                128 * col : 128 * col + 128, 128 * row : 128 * row + 128
            ].T
    parts[...] = as_right_rows(gram[...])

    def sweep(_, basis):
        return orthonormal(dot(as_left(basis), parts[...], NN))

    return lax.fori_loop(0, ITERS, sweep, start_ref[...])


def first_basis_kernel(
    core_ref, mine_ref, other_ref, start_ref, fibers_hbm, basis_ref, reduced_ref, whole, gram, parts, fibers, sem
):
    copy = pltpu.make_async_copy(fibers_hbm, fibers, sem)
    copy.start()
    basis = leading(core_ref, mine_ref, other_ref, start_ref, whole, gram, parts)
    basis_ref[...] = basis.T
    basis = as_left(basis)
    copy.wait()
    flat = fibers.reshape(N * 16, 128)
    out = reduced_ref.reshape(RANK * 16, 128)
    for j in range(0, 16, 2):
        pair = jnp.concatenate([flat[pl.ds(j, N, stride=16), :], flat[pl.ds(j + 1, N, stride=16), :]], axis=1)
        reduced = dot(basis, as_right_rows(pair), NN)
        out[pl.ds(j, RANK, stride=16), :] = reduced[:, :128]
        out[pl.ds(j + 1, RANK, stride=16), :] = reduced[:, 128:]


def second_basis_kernel(core_ref, mine_ref, other_ref, start_ref, slab_ref, basis_ref, core_out, whole, gram, parts):
    basis = leading(core_ref, mine_ref, other_ref, start_ref, whole, gram, parts)
    basis_ref[...] = basis.T
    basis = as_left(basis)
    for a in range(0, 4, 2):
        pair = jnp.concatenate([slab_ref[:, a].reshape(N, 128), slab_ref[:, a + 1].reshape(N, 128)], axis=1)
        got = dot(basis, as_right_rows(pair), NN)
        core_out[:, a] = got[:, :128].reshape(8, 16, 128)
        core_out[:, a + 1] = got[:, 128:].reshape(8, 16, 128)


def shaped(*shape):
    return jax.ShapeDtypeStruct(shape, F32)


def gram_call(kernel, depth, core, x):
    return pl.pallas_call(
        kernel,
        out_shape=(shaped(HALF, 8, 128), shaped(HALF, 8, 128)),
        in_specs=[SMEM, VMEM],
        out_specs=(VMEM, VMEM),
        scratch_shapes=[
            pltpu.VMEM((N, depth), BF16),
            pltpu.VMEM((N, depth), BF16),
            pltpu.VMEM((2, HALF, 8, 128), F32),
        ],
        compiler_params=PARAMS,
    )(core, x)


LEADING_SCRATCH = [
    pltpu.VMEM((2, HALF, 8, 128), F32),
    pltpu.VMEM((N, N), F32),
    pltpu.VMEM((3 * N, N), BF16),
]


def across_cores(x):
    return lax.ppermute(x, "c", [(0, 1), (1, 0)])


def total(mine, other):
    share = HALF // 16
    mine = (mine + across_cores(other)).reshape(16, share, 8, 128)
    got = jnp.sum(lax.all_to_all(mine, ("x", "y"), 0, 0, tiled=True), axis=0)
    got = jnp.sum(lax.all_to_all(jnp.broadcast_to(got, (8, share, 8, 128)), "z", 0, 0, tiled=True), axis=0)
    got = lax.all_to_all(jnp.broadcast_to(got, (16, share, 8, 128)), ("x", "y"), 0, 0, tiled=True)
    got = got.reshape(HALF, 8, 128)
    return got, across_cores(got)


def local(field, seeds_first, seeds_second):
    core = lax.axis_index("c").reshape(1)
    sent = field.reshape(16, 4, 16, 8, 128).transpose(3, 1, 0, 2, 4).reshape(32, 16, 16, 128)
    fibers = lax.all_to_all(sent, ("z", "x"), 0, 0, tiled=True).reshape(N, 16, 128)
    starts = pl.pallas_call(
        seeds_kernel, out_shape=(shaped(RANK, N), shaped(RANK, N)), compiler_params=PARAMS
    )(seeds_first.T, seeds_second.T)

    mine, other = total(*gram_call(first_gram_kernel, 2048, core, fibers))
    basis_first, reduced = pl.pallas_call(
        first_basis_kernel,
        out_shape=(shaped(N, RANK), shaped(RANK, 16, 128)),
        in_specs=[SMEM, VMEM, VMEM, VMEM, ANY],
        out_specs=(VMEM, VMEM),
        scratch_shapes=LEADING_SCRATCH + [pltpu.VMEM((N, 16, 128), F32), pltpu.SemaphoreType.DMA],
        compiler_params=PARAMS,
    )(core, mine, other, starts[0], fibers)

    slab = lax.all_to_all(reduced.reshape(32, 4, 16, 128), ("y", "c", "x"), 0, 0, tiled=True)
    mine, other = total(*gram_call(second_gram_kernel, 512, core, slab))
    basis_second, ranks = pl.pallas_call(
        second_basis_kernel,
        out_shape=(shaped(N, RANK), shaped(8, 4, 16, 128)),
        in_specs=[SMEM, VMEM, VMEM, VMEM, VMEM],
        out_specs=(VMEM, VMEM),
        scratch_shapes=LEADING_SCRATCH,
        compiler_params=PARAMS,
    )(core, mine, other, starts[1], slab)
    ranks = lax.all_to_all(ranks, ("y", "c"), 0, 0, tiled=True)
    ranks = lax.all_to_all(ranks, "z", 0, 0, tiled=True)
    core_tensor = ranks.transpose(1, 2, 0, 3).reshape(4, 16, 1024)
    return (basis_first, basis_second, core_tensor)


def solution(mesh):
    fine = Mesh(mesh.devices.reshape(8, 4, 4, 2), ("z", "x", "y", "c"))
    return jax.shard_map(
        local,
        mesh=fine,
        in_specs=(P(("z", "x"), ("y", "c"), None), P(), P()),
        out_specs=(P(), P(), P(("z", "x"), ("y", "c"), None)),
        check_vma=False,
    )
```

```python
import jax
import jax.numpy as jnp
from jax import lax
from jax.experimental import pallas as pl
from jax.experimental.pallas import tpu as pltpu
from jax.sharding import Mesh, PartitionSpec as P

ITERS = 4
N = 512
RANK = 128
F32 = jnp.float32
BF16 = jnp.bfloat16
NN = (((1,), (0,)), ((), ()))
NT = (((1,), (1,)), ((), ()))
TILES = [(row, col) for row in range(64) for col in range(row // 16, 4)]
HALF = len(TILES) // 2
PARAMS = pltpu.CompilerParams(vmem_limit_bytes=56 * 2**20)
VMEM = pl.BlockSpec(memory_space=pltpu.VMEM)
SMEM = pl.BlockSpec(memory_space=pltpu.SMEM)
ANY = pl.BlockSpec(memory_space=pl.ANY)


def dot(left, right, dims):
    return lax.dot_general(left, right, dims, preferred_element_type=F32)


def split(x):
    high = x.astype(BF16)
    return high, (x - high.astype(F32)).astype(BF16)


def as_left(x):
    high, low = split(x)
    return jnp.concatenate([high, low, high], axis=1)


def as_right_rows(x):
    high, low = split(x)
    return jnp.concatenate([high, high, low], axis=0)


def as_right_cols(x):
    high, low = split(x)
    return jnp.concatenate([high, high, low], axis=1)


def inverse_factor(inner):
    sub = lax.broadcasted_iota(jnp.int32, (8, RANK), 0)
    lane = lax.broadcasted_iota(jnp.int32, (8, RANK), 1)
    panels = RANK // 8
    left = [inner[8 * i : 8 * i + 8, :] for i in range(panels)]
    right = [jnp.where(lane == sub + 8 * i, 1.0, 0.0).astype(F32) for i in range(panels)]
    spread = lambda row: jnp.broadcast_to(row, (8, RANK))
    out = []
    for p in range(panels):
        rows = range(p, panels)
        cols = {i: [spread(left[i][:, 8 * p + t : 8 * p + t + 1]) for t in range(8)] for i in rows}
        done = jnp.zeros((8, RANK), F32)
        for t in range(8):
            root = lax.rsqrt(spread(cols[p][t][t : t + 1, :]))
            left_row = spread(left[p][t : t + 1, :]) * root
            right_row = spread(right[p][t : t + 1, :]) * root
            done = jnp.where(sub == t, right_row, done)
            ahead = [spread(cols[p][u][t : t + 1, :]) * root for u in range(t + 1, 8)]
            for i in rows:
                factor = cols[i][t] * root
                left[i] = left[i] - factor * left_row
                right[i] = right[i] - factor * right_row
                for k, u in enumerate(range(t + 1, 8)):
                    cols[i][u] = cols[i][u] - factor * ahead[k]
        out.append(done)
    return jnp.concatenate(out, axis=0)


def orthonormal(turned):
    inner = dot(as_left(turned), as_right_cols(turned), NT)
    return dot(as_left(inverse_factor(inner)), as_right_rows(turned), NN)


def seeds_kernel(first_ref, second_ref, first_out, second_out):
    first_out[...] = orthonormal(first_ref[...].astype(F32))
    second_out[...] = orthonormal(second_ref[...].astype(F32))


def upper_gram(high, low, mine_ref, other_ref, swap, core):
    for block in range(4):
        rows = slice(128 * block, 128 * block + 128)
        cols = slice(128 * block, N)
        gram = dot(
            jnp.concatenate([high[rows, :], low[rows, :], high[rows, :]], axis=1),
            jnp.concatenate([high[cols, :], high[cols, :], low[cols, :]], axis=1),
            NT,
        )
        for at, (row, col) in enumerate(TILES):
            if row // 16 == block:
                r, c = 8 * (row % 16), 128 * (col - block)
                half = lax.bitwise_xor(at // HALF, core)
                swap[half, at % HALF] = gram[r : r + 8, c : c + 128]
    mine_ref[...] = swap[0]
    other_ref[...] = swap[1]


def pack_kernel(field_ref, out_ref):
    for i in range(8):
        block = jnp.concatenate([field_ref[0, i], field_ref[1, i]], axis=0)
        out_ref[0, :, 0, i, :] = block.T


def first_gram_kernel(core_ref, fibers_hbm, mine_ref, other_ref, high_hbm, low_hbm, fibers, high, low, swap, sems, out_sems):
    copies = [pltpu.make_async_copy(fibers_hbm.at[:, :, p], fibers.at[p], sems.at[p]) for p in range(4)]
    for copy in copies:
        copy.start()
    first_half = lax.broadcasted_iota(jnp.int32, (32, 8, 128), 2) < 64
    for p in range(4):
        copies[p].wait()
        for pair in range(4):
            one, two = fibers[p, :, 2 * pair], fibers[p, :, 2 * pair + 1]
            upper = jnp.where(first_half, one, pltpu.roll(two, 64, 2))
            lower = jnp.where(first_half, pltpu.roll(one, 64, 2), two)
            h, l = split(jnp.stack([upper, lower], axis=1).reshape(N, 128))
            at = slice(512 * p + 128 * pair, 512 * p + 128 * pair + 128)
            high[:, at] = h
            low[:, at] = l
    saves = [
        pltpu.make_async_copy(high, high_hbm, out_sems.at[0]),
        pltpu.make_async_copy(low, low_hbm, out_sems.at[1]),
    ]
    for save in saves:
        save.start()
    upper_gram(high, low, mine_ref, other_ref, swap, core_ref[0])
    for save in saves:
        save.wait()


def leading(core_ref, mine_ref, other_ref, start_ref, whole, gram, parts):
    core = core_ref[0]
    whole[core] = mine_ref[...]
    whole[1 - core] = other_ref[...]
    for at, (row, col) in enumerate(TILES):
        gram[8 * row : 8 * row + 8, 128 * col : 128 * col + 128] = whole[at // HALF, at % HALF]
    for row in range(1, 4):
        for col in range(row):
            gram[128 * row : 128 * row + 128, 128 * col : 128 * col + 128] = gram[
                128 * col : 128 * col + 128, 128 * row : 128 * row + 128
            ].T
    parts[...] = as_right_rows(gram[...])

    def sweep(_, basis):
        return orthonormal(dot(as_left(basis), parts[...], NN))

    return lax.fori_loop(0, ITERS, sweep, start_ref[...])


def first_basis_kernel(
    core_ref, mine_ref, other_ref, start_ref, high_hbm, low_hbm,
    basis_ref, reduced_ref, mine_out, other_out,
    whole, gram, parts, held, high, low, turned_high, turned_low, sems,
):
    copies = [pltpu.make_async_copy(high_hbm, high, sems.at[0]), pltpu.make_async_copy(low_hbm, low, sems.at[1])]
    for copy in copies:
        copy.start()
    basis = leading(core_ref, mine_ref, other_ref, start_ref, whole, gram, parts)
    basis_ref[...] = basis.T
    columns = []
    for k in range(4):
        held[k] = basis[:, 128 * k : 128 * k + 128]
        columns.append(jnp.concatenate([held[k, pl.ds(r, 32, stride=4), :] for r in range(4)], axis=0))
    basis = jnp.concatenate(columns, axis=1)
    basis_high, basis_low = split(basis)
    both = jnp.concatenate([basis_high, basis_low], axis=0)
    for copy in copies:
        copy.wait()
    for p in range(4):
        at = slice(512 * p, 512 * p + 512)
        twice = dot(both, high[:, at], NN)
        reduced = twice[:RANK] + twice[RANK:] + dot(basis_high, low[:, at], NN)
        reduced_ref[:, at] = reduced
        h, l = split(reduced.T)
        turned_high[:, 128 * p : 128 * p + 128] = h
        turned_low[:, 128 * p : 128 * p + 128] = l
    upper_gram(turned_high, turned_low, mine_out, other_out, whole, core_ref[0])


def second_basis_kernel(
    core_ref, mine_ref, other_ref, start_ref, reduced_hbm, basis_ref, core_out, whole, gram, parts, reduced, product, sem
):
    copy = pltpu.make_async_copy(reduced_hbm, reduced, sem)
    copy.start()
    basis = leading(core_ref, mine_ref, other_ref, start_ref, whole, gram, parts)
    basis_ref[...] = basis.T
    basis = as_right_cols(basis)
    copy.wait()
    for p in range(4):
        product[128 * p : 128 * p + 128, :] = dot(as_left(reduced[:, 512 * p : 512 * p + 512]), basis, NT)
    row = lax.broadcasted_iota(jnp.int32, (8, 128), 0)
    group = lax.broadcasted_iota(jnp.int32, (8, 128), 1) // 16
    for q in range(32):
        for half in range(2):
            block = product[pl.ds(q + 256 * half, 8, stride=32), :]
            for bit in (1, 2, 4):
                up = pltpu.roll(pltpu.roll(block, 8 - bit, 0), 16 * bit, 1)
                down = pltpu.roll(pltpu.roll(block, bit, 0), 128 - 16 * bit, 1)
                same = (row & bit) == (group & bit)
                block = jnp.where(same, block, jnp.where((row & bit) == 0, up, down))
            core_out[pl.ds(16 * q + half, 8, stride=2), :] = block


def unpack_kernel(got_ref, out_ref):
    for half in range(2):
        for part in range(2):
            block = got_ref[pl.ds(256 * part + half, 128, stride=2), :].T
            for low in range(2):
                at = 256 * (2 * half + low) + 128 * part
                out_ref[:, :, at : at + 128] = block[64 * low : 64 * low + 64].reshape(4, 16, 128)


def shaped(*shape):
    return jax.ShapeDtypeStruct(shape, F32)


def shaped_half(*shape):
    return jax.ShapeDtypeStruct(shape, BF16)


LEADING_SCRATCH = [
    pltpu.VMEM((2, HALF, 8, 128), F32),
    pltpu.VMEM((N, N), F32),
    pltpu.VMEM((3 * N, N), BF16),
]


def across_cores(x):
    return lax.ppermute(x, "c", [(0, 1), (1, 0)])


def total(mine, other):
    share = HALF // 16
    mine = (mine + across_cores(other)).reshape(16, share, 8, 128)
    got = jnp.sum(lax.all_to_all(mine, ("x", "y"), 0, 0, tiled=True), axis=0)
    got = jnp.sum(lax.all_to_all(jnp.broadcast_to(got, (8, share, 8, 128)), "z", 0, 0, tiled=True), axis=0)
    got = lax.all_to_all(jnp.broadcast_to(got, (16, share, 8, 128)), ("x", "y"), 0, 0, tiled=True)
    got = got.reshape(HALF, 8, 128)
    return got, across_cores(got)


def local(field, seeds_first, seeds_second):
    core = lax.axis_index("c").reshape(1)
    sent = pl.pallas_call(
        pack_kernel,
        grid=(4, 2),
        out_shape=shaped(2, 128, 4, 8, 128),
        in_specs=[pl.BlockSpec((2, 8, 64, 128), lambda p, h: (0, 0, 0, 2 * p + h))],
        out_specs=pl.BlockSpec((1, 128, 1, 8, 128), lambda p, h: (h, 0, p, 0, 0)),
        compiler_params=PARAMS,
    )(field.reshape(2, 8, 64, 1024))
    fibers = lax.all_to_all(sent.reshape(256, 4, 8, 128), ("z", "x", "y", "c"), 0, 0, tiled=True)
    starts = pl.pallas_call(
        seeds_kernel, out_shape=(shaped(RANK, N), shaped(RANK, N)), compiler_params=PARAMS
    )(seeds_first.T, seeds_second.T)
    fibers, starts = lax.optimization_barrier((fibers, starts))

    halves = (shaped(HALF, 8, 128), shaped(HALF, 8, 128))
    mine, other, high, low = pl.pallas_call(
        first_gram_kernel,
        out_shape=halves + (shaped_half(N, 2048), shaped_half(N, 2048)),
        in_specs=[SMEM, ANY],
        out_specs=(VMEM, VMEM, ANY, ANY),
        scratch_shapes=[
            pltpu.VMEM((4, 32, 8, 8, 128), F32),
            pltpu.VMEM((N, 2048), BF16),
            pltpu.VMEM((N, 2048), BF16),
            pltpu.VMEM((2, HALF, 8, 128), F32),
            pltpu.SemaphoreType.DMA((4,)),
            pltpu.SemaphoreType.DMA((2,)),
        ],
        compiler_params=PARAMS,
    )(core, fibers.reshape(32, 8, 4, 8, 128))
    mine, other = total(mine, other)
    basis_first, reduced, mine, other = pl.pallas_call(
        first_basis_kernel,
        out_shape=(shaped(N, RANK), shaped(RANK, 2048)) + halves,
        in_specs=[SMEM, VMEM, VMEM, VMEM, ANY, ANY],
        out_specs=(VMEM, VMEM, VMEM, VMEM),
        scratch_shapes=LEADING_SCRATCH
        + [
            pltpu.VMEM((4, RANK, 128), F32),
            pltpu.VMEM((N, 2048), BF16),
            pltpu.VMEM((N, 2048), BF16),
            pltpu.VMEM((N, 4 * RANK), BF16),
            pltpu.VMEM((N, 4 * RANK), BF16),
            pltpu.SemaphoreType.DMA((2,)),
        ],
        compiler_params=PARAMS,
    )(core, mine, other, starts[0], high, low)
    mine, other = total(mine, other)
    basis_second, ranks = pl.pallas_call(
        second_basis_kernel,
        out_shape=(shaped(N, RANK), shaped(512, 128)),
        in_specs=[SMEM, VMEM, VMEM, VMEM, ANY],
        out_specs=(VMEM, VMEM),
        scratch_shapes=LEADING_SCRATCH
        + [pltpu.VMEM((RANK, 2048), F32), pltpu.VMEM((4 * RANK, RANK), F32), pltpu.SemaphoreType.DMA],
        compiler_params=PARAMS,
    )(core, mine, other, starts[1], reduced)
    ranks = lax.all_to_all(ranks.reshape(256, 2, 128), ("z", "x", "y", "c"), 0, 0, tiled=True)
    core_tensor = pl.pallas_call(unpack_kernel, out_shape=shaped(4, 16, 1024), compiler_params=PARAMS)(
        ranks.reshape(512, 128)
    )
    return (basis_first, basis_second, core_tensor)


def solution(mesh):
    fine = Mesh(mesh.devices.reshape(8, 4, 4, 2), ("z", "x", "y", "c"))
    return jax.shard_map(
        local,
        mesh=fine,
        in_specs=(P(("z", "x"), ("y", "c"), None), P(), P()),
        out_specs=(P(), P(), P(("z", "x"), ("y", "c"), None)),
        check_vma=False,
    )
```

```python
import jax
import jax.numpy as jnp
from jax import lax
from jax.experimental import pallas as pl
from jax.experimental.pallas import tpu as pltpu
from jax.sharding import Mesh, PartitionSpec as P

ITERS = 4
N = 512
RANK = 128
F32 = jnp.float32
BF16 = jnp.bfloat16
NN = (((1,), (0,)), ((), ()))
NT = (((1,), (1,)), ((), ()))
TILES = [(row, col) for row in range(64) for col in range(row // 16, 4)]
HALF = len(TILES) // 2
PARAMS = pltpu.CompilerParams(vmem_limit_bytes=56 * 2**20)
VMEM = pl.BlockSpec(memory_space=pltpu.VMEM)
SMEM = pl.BlockSpec(memory_space=pltpu.SMEM)
ANY = pl.BlockSpec(memory_space=pl.ANY)


def dot(left, right, dims):
    return lax.dot_general(left, right, dims, preferred_element_type=F32)


def split(x):
    high = x.astype(BF16)
    return high, (x - high.astype(F32)).astype(BF16)


def as_left(x):
    high, low = split(x)
    return jnp.concatenate([high, low, high], axis=1)


def as_right_rows(x):
    high, low = split(x)
    return jnp.concatenate([high, high, low], axis=0)


def as_right_cols(x):
    high, low = split(x)
    return jnp.concatenate([high, high, low], axis=1)


def inverse_factor(inner, one):
    sub = lax.broadcasted_iota(jnp.int32, (8, RANK), 0)
    lane = lax.broadcasted_iota(jnp.int32, (8, RANK), 1)
    spread = lambda row: jnp.broadcast_to(row, (8, RANK))
    rest = [inner[8 * i : 8 * i + 8, :] for i in range(RANK // 8)]
    out = []
    for last in (8, 16):
        factor = []
        for p in range(last - 8, last):
            rows = range(p, last)
            cols = {i: [spread(rest[i][:, 8 * p + t : 8 * p + t + 1]) for t in range(8)] for i in rows}
            cols[p] = [col * one for col in cols[p]]
            panel = (lane >= 8 * p) & (lane < 8 * p + 8)
            for i in rows:
                unit = jnp.where(lane == sub + 8 * p, 1.0, 0.0) if i == p else 0.0
                rest[i] = jnp.where(panel, unit, rest[i])
            done = jnp.zeros((8, RANK), F32)
            pivots = jnp.ones((8, RANK), F32)
            for t in range(8):
                pivot = spread(cols[p][t][t : t + 1, :])
                row = spread(rest[p][t : t + 1, :])
                done = jnp.where(sub == t, row, done)
                pivots = jnp.where(sub == t, pivot, pivots)
                inverse = 1.0 / pivot
                ahead = [spread(cols[p][u][t : t + 1, :]) for u in range(t + 1, 8)]
                for i in rows:
                    scaled = cols[i][t] * inverse
                    for k, u in enumerate(range(t + 1, 8)):
                        cols[i][u] = cols[i][u] - scaled * ahead[k]
                    if i > p or t < 7:
                        rest[i] = rest[i] - scaled * row
            done = done * lax.rsqrt(pivots)
            out.append(jnp.where(lane < 8 * p + 8, done, 0.0))
            factor.append(jnp.where((lane < 8 * p + 8) | (lane >= 8 * last), done, 0.0))
        if last < 16:
            factor = jnp.concatenate(factor, axis=0)
            change = lax.dot_general(
                factor[:, 8 * last :],
                factor,
                (((0,), (0,)), ((), ())),
                precision=lax.Precision.HIGHEST,
                preferred_element_type=F32,
            )
            for k, i in enumerate(range(last, 16)):
                rest[i] = jnp.where(lane < 8 * last, 0.0, rest[i]) - change[8 * k : 8 * k + 8]
    return jnp.concatenate(out, axis=0)


def ones(core_ref):
    return jnp.full((8, RANK), jnp.minimum(core_ref[0] + 1, 1).astype(F32))


def orthonormal(turned, one):
    inner = dot(as_left(turned), as_right_cols(turned), NT)
    return dot(as_left(inverse_factor(inner, one)), as_right_rows(turned), NN)


def seeds_kernel(core_ref, first_ref, second_ref, first_out, second_out):
    one = ones(core_ref)
    first_out[...] = orthonormal(first_ref[...].astype(F32), one)
    second_out[...] = orthonormal(second_ref[...].astype(F32), one)


def upper_gram(high, low, mine_ref, other_ref, swap, core):
    for block in range(2):
        rows, cols = slice(0, 256 * block + 256), slice(256 * block, 256 * block + 256)
        gram = dot(high[rows, :], high[cols, :], NT)
        gram += dot(low[rows, :], high[cols, :], NT)
        gram += dot(high[rows, :], low[cols, :], NT)
        for at, (row, col) in enumerate(TILES):
            if col // 2 == block:
                r, c = 8 * row, 128 * (col % 2)
                half = lax.bitwise_xor(at // HALF, core)
                swap[half, at % HALF] = gram[r : r + 8, c : c + 128]
    mine_ref[...] = swap[0]
    other_ref[...] = swap[1]


def pack_kernel(field_hbm, out_hbm, field, out, sems, out_sems):
    copies = [pltpu.make_async_copy(field_hbm.at[:, i], field.at[:, i], sems.at[i]) for i in range(8)]
    for copy in copies:
        copy.start()
    saves = []
    for half in range(2):
        for i in range(8):
            if half == 0:
                copies[i].wait()
            for p in range(4):
                at = slice(256 * p + 128 * half, 256 * p + 128 * half + 128)
                out[half, :, p, i, :] = jnp.concatenate([field[0, i, :, at], field[1, i, :, at]], axis=0).T
        saves.append(pltpu.make_async_copy(out.at[half], out_hbm.at[half], out_sems.at[half]))
        saves[half].start()
    for save in saves:
        save.wait()


def first_gram_kernel(core_ref, fibers_hbm, mine_ref, other_ref, high_hbm, low_hbm, fibers, high, low, swap, sems, out_sems):
    quarters = [slice(8 * q, 8 * q + 8) for q in range(4)]
    copies = [pltpu.make_async_copy(fibers_hbm.at[at], fibers.at[at], sems.at[q]) for q, at in enumerate(quarters)]
    for copy in copies:
        copy.start()
    first_half = lax.broadcasted_iota(jnp.int32, (8, 8, 128), 2) < 64
    for q in range(4):
        copies[q].wait()
        for p in range(4):
            for pair in range(4):
                one, two = fibers[quarters[q], 2 * pair, p], fibers[quarters[q], 2 * pair + 1, p]
                upper = jnp.where(first_half, one, pltpu.roll(two, 64, 2))
                lower = jnp.where(first_half, pltpu.roll(one, 64, 2), two)
                h, l = split(jnp.stack([upper, lower], axis=1).reshape(128, 128))
                at = slice(512 * p + 128 * pair, 512 * p + 128 * pair + 128)
                high[128 * q : 128 * q + 128, at] = h
                low[128 * q : 128 * q + 128, at] = l
    saves = [
        pltpu.make_async_copy(high, high_hbm, out_sems.at[0]),
        pltpu.make_async_copy(low, low_hbm, out_sems.at[1]),
    ]
    for save in saves:
        save.start()
    upper_gram(high, low, mine_ref, other_ref, swap, core_ref[0])
    for save in saves:
        save.wait()


def leading(core_ref, mine_hbm, other_hbm, start_ref, whole, gram, parts, tile_sems):
    core = core_ref[0]
    one = ones(core_ref)
    copies = [
        pltpu.make_async_copy(mine_hbm, whole.at[core], tile_sems.at[0]),
        pltpu.make_async_copy(other_hbm, whole.at[1 - core], tile_sems.at[1]),
    ]
    for copy in copies:
        copy.start()
    for copy in copies:
        copy.wait()
    for at, (row, col) in enumerate(TILES):
        gram[8 * row : 8 * row + 8, 128 * col : 128 * col + 128] = whole[at // HALF, at % HALF]
    for row in range(1, 4):
        for col in range(row):
            gram[128 * row : 128 * row + 128, 128 * col : 128 * col + 128] = gram[
                128 * col : 128 * col + 128, 128 * row : 128 * row + 128
            ].T
    parts[...] = as_right_rows(gram[...])

    def sweep(_, basis):
        return orthonormal(dot(as_left(basis), parts[...], NN), one)

    return lax.fori_loop(0, ITERS, sweep, start_ref[...])


def first_basis_kernel(
    core_ref, mine_ref, other_ref, start_ref, high_hbm, low_hbm,
    basis_ref, reduced_ref, mine_out, other_out,
    whole, gram, parts, tile_sems, held, high, low, turned_high, turned_low, sems,
):
    copies = [pltpu.make_async_copy(high_hbm, high, sems.at[0]), pltpu.make_async_copy(low_hbm, low, sems.at[1])]
    for copy in copies:
        copy.start()
    basis = leading(core_ref, mine_ref, other_ref, start_ref, whole, gram, parts, tile_sems)
    basis_ref[...] = basis.T
    columns = []
    for k in range(4):
        held[k] = basis[:, 128 * k : 128 * k + 128]
        columns.append(jnp.concatenate([held[k, pl.ds(r, 32, stride=4), :] for r in range(4)], axis=0))
    basis = jnp.concatenate(columns, axis=1)
    basis_high, basis_low = split(basis)
    both = jnp.concatenate([basis_high, basis_low], axis=0)
    for copy in copies:
        copy.wait()
    for p in range(4):
        at = slice(512 * p, 512 * p + 512)
        twice = dot(both, high[:, at], NN)
        reduced = twice[:RANK] + twice[RANK:] + dot(basis_high, low[:, at], NN)
        reduced_ref[:, at] = reduced
        h, l = split(reduced.T)
        turned_high[:, 128 * p : 128 * p + 128] = h
        turned_low[:, 128 * p : 128 * p + 128] = l
    upper_gram(turned_high, turned_low, mine_out, other_out, whole, core_ref[0])


def second_basis_kernel(
    core_ref, mine_ref, other_ref, start_ref, reduced_hbm, basis_ref, core_out,
    whole, gram, parts, tile_sems, reduced, product, sem
):
    copy = pltpu.make_async_copy(reduced_hbm, reduced, sem)
    copy.start()
    basis = leading(core_ref, mine_ref, other_ref, start_ref, whole, gram, parts, tile_sems)
    basis_ref[...] = basis.T
    basis = as_right_cols(basis)
    copy.wait()
    for p in range(4):
        product[128 * p : 128 * p + 128, :] = dot(as_left(reduced[:, 512 * p : 512 * p + 512]), basis, NT)
    row = lax.broadcasted_iota(jnp.int32, (8, 128), 0)
    group = lax.broadcasted_iota(jnp.int32, (8, 128), 1) // 16
    for q in range(32):
        for half in range(2):
            block = product[pl.ds(q + 256 * half, 8, stride=32), :]
            for bit in (1, 2, 4):
                up = pltpu.roll(pltpu.roll(block, 8 - bit, 0), 16 * bit, 1)
                down = pltpu.roll(pltpu.roll(block, bit, 0), 128 - 16 * bit, 1)
                same = (row & bit) == (group & bit)
                block = jnp.where(same, block, jnp.where((row & bit) == 0, up, down))
            core_out[pl.ds(16 * q + half, 8, stride=2), :] = block


def unpack_kernel(got_ref, out_ref):
    for half in range(2):
        for part in range(2):
            block = got_ref[pl.ds(256 * part + half, 128, stride=2), :].T
            for low in range(2):
                at = 256 * (2 * half + low) + 128 * part
                out_ref[:, :, at : at + 128] = block[64 * low : 64 * low + 64].reshape(4, 16, 128)


def shaped(*shape):
    return jax.ShapeDtypeStruct(shape, F32)


def shaped_half(*shape):
    return jax.ShapeDtypeStruct(shape, BF16)


LEADING_SCRATCH = [
    pltpu.VMEM((2, HALF, 8, 128), F32),
    pltpu.VMEM((N, N), F32),
    pltpu.VMEM((3 * N, N), BF16),
    pltpu.SemaphoreType.DMA((2,)),
]


def across_cores(x):
    return lax.ppermute(x, "c", [(0, 1), (1, 0)])


def total(mine, other):
    share = HALF // 16
    mine = (mine + across_cores(other)).reshape(16, share, 8, 128)
    got = jnp.sum(lax.all_to_all(mine, ("x", "y"), 0, 0, tiled=True), axis=0)
    got = jnp.sum(lax.all_to_all(jnp.broadcast_to(got, (8, share, 8, 128)), "z", 0, 0, tiled=True), axis=0)
    got = lax.all_to_all(jnp.broadcast_to(got, (16, share, 8, 128)), ("x", "y"), 0, 0, tiled=True)
    got = got.reshape(HALF, 8, 128)
    return got, across_cores(got)


def local(field, seeds_first, seeds_second):
    core = lax.axis_index("c").reshape(1)
    sent = pl.pallas_call(
        pack_kernel,
        out_shape=shaped(2, 128, 4, 8, 128),
        in_specs=[ANY],
        out_specs=ANY,
        scratch_shapes=[
            pltpu.VMEM((2, 8, 64, 1024), F32),
            pltpu.VMEM((2, 128, 4, 8, 128), F32),
            pltpu.SemaphoreType.DMA((8,)),
            pltpu.SemaphoreType.DMA((2,)),
        ],
        compiler_params=PARAMS,
    )(field.reshape(2, 8, 64, 1024))
    fibers = lax.all_to_all(sent.reshape(256, 4, 8, 128), ("z", "x", "y", "c"), 0, 0, tiled=True)
    starts = pl.pallas_call(
        seeds_kernel,
        out_shape=(shaped(RANK, N), shaped(RANK, N)),
        in_specs=[SMEM, VMEM, VMEM],
        compiler_params=PARAMS,
    )(core, seeds_first.T, seeds_second.T)
    fibers, starts = lax.optimization_barrier((fibers, starts))

    halves = (shaped(HALF, 8, 128), shaped(HALF, 8, 128))
    mine, other, high, low = pl.pallas_call(
        first_gram_kernel,
        out_shape=halves + (shaped_half(N, 2048), shaped_half(N, 2048)),
        in_specs=[SMEM, ANY],
        out_specs=(VMEM, VMEM, ANY, ANY),
        scratch_shapes=[
            pltpu.VMEM((32, 8, 4, 8, 128), F32),
            pltpu.VMEM((N, 2048), BF16),
            pltpu.VMEM((N, 2048), BF16),
            pltpu.VMEM((2, HALF, 8, 128), F32),
            pltpu.SemaphoreType.DMA((4,)),
            pltpu.SemaphoreType.DMA((2,)),
        ],
        compiler_params=PARAMS,
    )(core, fibers.reshape(32, 8, 4, 8, 128))
    mine, other = total(mine, other)
    basis_first, reduced, mine, other = pl.pallas_call(
        first_basis_kernel,
        out_shape=(shaped(N, RANK), shaped(RANK, 2048)) + halves,
        in_specs=[SMEM, ANY, ANY, VMEM, ANY, ANY],
        out_specs=(VMEM, VMEM, VMEM, VMEM),
        scratch_shapes=LEADING_SCRATCH
        + [
            pltpu.VMEM((4, RANK, 128), F32),
            pltpu.VMEM((N, 2048), BF16),
            pltpu.VMEM((N, 2048), BF16),
            pltpu.VMEM((N, 4 * RANK), BF16),
            pltpu.VMEM((N, 4 * RANK), BF16),
            pltpu.SemaphoreType.DMA((2,)),
        ],
        compiler_params=PARAMS,
    )(core, mine, other, starts[0], high, low)
    mine, other = total(mine, other)
    basis_second, ranks = pl.pallas_call(
        second_basis_kernel,
        out_shape=(shaped(N, RANK), shaped(512, 128)),
        in_specs=[SMEM, ANY, ANY, VMEM, ANY],
        out_specs=(VMEM, VMEM),
        scratch_shapes=LEADING_SCRATCH
        + [pltpu.VMEM((RANK, 2048), F32), pltpu.VMEM((4 * RANK, RANK), F32), pltpu.SemaphoreType.DMA],
        compiler_params=PARAMS,
    )(core, mine, other, starts[1], reduced)
    ranks = lax.all_to_all(ranks.reshape(256, 2, 128), ("z", "x", "y", "c"), 0, 0, tiled=True)
    core_tensor = pl.pallas_call(unpack_kernel, out_shape=shaped(4, 16, 1024), compiler_params=PARAMS)(
        ranks.reshape(512, 128)
    )
    return (basis_first, basis_second, core_tensor)


def solution(mesh):
    fine = Mesh(mesh.devices.reshape(8, 4, 4, 2), ("z", "x", "y", "c"))
    return jax.shard_map(
        local,
        mesh=fine,
        in_specs=(P(("z", "x"), ("y", "c"), None), P(), P()),
        out_specs=(P(), P(), P(("z", "x"), ("y", "c"), None)),
        check_vma=False,
    )
```

```python
import jax
import jax.numpy as jnp
from jax import lax
from jax.experimental import pallas as pl
from jax.experimental.pallas import tpu as pltpu
from jax.sharding import Mesh, PartitionSpec as P

ITERS = 4
N = 512
RANK = 128
F32 = jnp.float32
BF16 = jnp.bfloat16
NN = (((1,), (0,)), ((), ()))
NT = (((1,), (1,)), ((), ()))
TILES = [(row, col) for row in range(64) for col in range(row // 16, 4)]
HALF = len(TILES) // 2
PARAMS = pltpu.CompilerParams(vmem_limit_bytes=56 * 2**20)
VMEM = pl.BlockSpec(memory_space=pltpu.VMEM)
SMEM = pl.BlockSpec(memory_space=pltpu.SMEM)
ANY = pl.BlockSpec(memory_space=pl.ANY)


def dot(left, right, dims):
    return lax.dot_general(left, right, dims, preferred_element_type=F32)


def split(x):
    high = x.astype(BF16)
    return high, (x - high.astype(F32)).astype(BF16)


def as_left(x):
    high, low = split(x)
    return jnp.concatenate([high, low, high], axis=1)


def as_right_rows(x):
    high, low = split(x)
    return jnp.concatenate([high, high, low], axis=0)


def as_right_cols(x):
    high, low = split(x)
    return jnp.concatenate([high, high, low], axis=1)


def inverse_factor(inner, one):
    sub = lax.broadcasted_iota(jnp.int32, (8, RANK), 0)
    lane = lax.broadcasted_iota(jnp.int32, (8, RANK), 1)
    spread = lambda row: jnp.broadcast_to(row, (8, RANK))
    rest = [inner[8 * i : 8 * i + 8, :] for i in range(RANK // 8)]
    out = []
    for last in (8, 16):
        factor = []
        for p in range(last - 8, last):
            rows = range(p, last)
            cols = {i: [spread(rest[i][:, 8 * p + t : 8 * p + t + 1]) for t in range(8)] for i in rows}
            cols[p] = [col * one for col in cols[p]]
            panel = (lane >= 8 * p) & (lane < 8 * p + 8)
            for i in rows:
                unit = jnp.where(lane == sub + 8 * p, 1.0, 0.0) if i == p else 0.0
                rest[i] = jnp.where(panel, unit, rest[i])
            done = jnp.zeros((8, RANK), F32)
            pivots = jnp.ones((8, RANK), F32)
            for t in range(8):
                pivot = spread(cols[p][t][t : t + 1, :])
                row = spread(rest[p][t : t + 1, :])
                done = jnp.where(sub == t, row, done)
                pivots = jnp.where(sub == t, pivot, pivots)
                inverse = 1.0 / pivot
                ahead = [spread(cols[p][u][t : t + 1, :]) for u in range(t + 1, 8)]
                for i in rows:
                    scaled = cols[i][t] * inverse
                    for k, u in enumerate(range(t + 1, 8)):
                        cols[i][u] = cols[i][u] - scaled * ahead[k]
                    if i > p or t < 7:
                        rest[i] = rest[i] - scaled * row
            done = done * lax.rsqrt(pivots)
            out.append(jnp.where(lane < 8 * p + 8, done, 0.0))
            factor.append(jnp.where((lane < 8 * p + 8) | (lane >= 8 * last), done, 0.0))
        if last < 16:
            factor = jnp.concatenate(factor, axis=0)
            change = lax.dot_general(
                factor[:, 8 * last :],
                factor,
                (((0,), (0,)), ((), ())),
                precision=lax.Precision.HIGHEST,
                preferred_element_type=F32,
            )
            for k, i in enumerate(range(last, 16)):
                rest[i] = jnp.where(lane < 8 * last, 0.0, rest[i]) - change[8 * k : 8 * k + 8]
    return jnp.concatenate(out, axis=0)


def ones(core_ref):
    return jnp.full((8, RANK), jnp.minimum(core_ref[0] + 1, 1).astype(F32))


def orthonormal(turned, one):
    inner = dot(as_left(turned), as_right_cols(turned), NT)
    return dot(as_left(inverse_factor(inner, one)), as_right_rows(turned), NN)


def seeds_kernel(core_ref, first_ref, second_ref, first_out, second_out):
    one = ones(core_ref)
    first_out[...] = orthonormal(first_ref[...].astype(F32), one)
    second_out[...] = orthonormal(second_ref[...].astype(F32), one)


def upper_gram(high, low, mine_ref, other_ref, swap, core):
    for block in range(2):
        rows, cols = slice(0, 256 * block + 256), slice(256 * block, 256 * block + 256)
        gram = dot(high[rows, :], high[cols, :], NT)
        gram += dot(low[rows, :], high[cols, :], NT)
        gram += dot(high[rows, :], low[cols, :], NT)
        for at, (row, col) in enumerate(TILES):
            if col // 2 == block:
                r, c = 8 * row, 128 * (col % 2)
                half = lax.bitwise_xor(at // HALF, core)
                swap[half, at % HALF] = gram[r : r + 8, c : c + 128]
    mine_ref[...] = swap[0]
    other_ref[...] = swap[1]


def pack_kernel(field_hbm, out_hbm, field, out, sems, out_sems):
    copies = [pltpu.make_async_copy(field_hbm.at[:, i], field.at[:, i], sems.at[i]) for i in range(8)]
    for copy in copies:
        copy.start()
    saves = []
    for half in range(2):
        for i in range(8):
            if half == 0:
                copies[i].wait()
            for p in range(4):
                at = slice(256 * p + 128 * half, 256 * p + 128 * half + 128)
                out[half, :, p, i, :] = jnp.concatenate([field[0, i, :, at], field[1, i, :, at]], axis=0).T
        saves.append(pltpu.make_async_copy(out.at[half], out_hbm.at[half], out_sems.at[half]))
        saves[half].start()
    for save in saves:
        save.wait()


def first_gram_kernel(core_ref, fibers_hbm, mine_ref, other_ref, high_hbm, low_hbm, fibers, high, low, swap, sems, out_sems):
    quarters = [slice(8 * q, 8 * q + 8) for q in range(4)]
    copies = [pltpu.make_async_copy(fibers_hbm.at[at], fibers.at[at], sems.at[q]) for q, at in enumerate(quarters)]
    for copy in copies:
        copy.start()
    first_half = lax.broadcasted_iota(jnp.int32, (8, 8, 128), 2) < 64
    for q in range(4):
        copies[q].wait()
        for p in range(4):
            for pair in range(4):
                one, two = fibers[quarters[q], 2 * pair, p], fibers[quarters[q], 2 * pair + 1, p]
                upper = jnp.where(first_half, one, pltpu.roll(two, 64, 2))
                lower = jnp.where(first_half, pltpu.roll(one, 64, 2), two)
                h, l = split(jnp.stack([upper, lower], axis=1).reshape(128, 128))
                at = slice(512 * p + 128 * pair, 512 * p + 128 * pair + 128)
                high[128 * q : 128 * q + 128, at] = h
                low[128 * q : 128 * q + 128, at] = l
    saves = [
        pltpu.make_async_copy(high, high_hbm, out_sems.at[0]),
        pltpu.make_async_copy(low, low_hbm, out_sems.at[1]),
    ]
    for save in saves:
        save.start()
    upper_gram(high, low, mine_ref, other_ref, swap, core_ref[0])
    for save in saves:
        save.wait()


def leading(core_ref, mine_ref, other_ref, start_ref, whole, gram, parts):
    core = core_ref[0]
    one = ones(core_ref)
    whole[core] = mine_ref[...]
    whole[1 - core] = other_ref[...]
    for at, (row, col) in enumerate(TILES):
        gram[8 * row : 8 * row + 8, 128 * col : 128 * col + 128] = whole[at // HALF, at % HALF]
    for row in range(1, 4):
        for col in range(row):
            gram[128 * row : 128 * row + 128, 128 * col : 128 * col + 128] = gram[
                128 * col : 128 * col + 128, 128 * row : 128 * row + 128
            ].T
    parts[...] = as_right_rows(gram[...])

    def sweep(_, basis):
        return orthonormal(dot(as_left(basis), parts[...], NN), one)

    return lax.fori_loop(0, ITERS, sweep, start_ref[...])


def first_basis_kernel(
    core_ref, mine_ref, other_ref, start_ref, high_hbm, low_hbm,
    basis_ref, reduced_ref, mine_out, other_out,
    whole, gram, parts, held, high, low, turned_high, turned_low, sems,
):
    copies = [pltpu.make_async_copy(high_hbm, high, sems.at[0]), pltpu.make_async_copy(low_hbm, low, sems.at[1])]
    for copy in copies:
        copy.start()
    basis = leading(core_ref, mine_ref, other_ref, start_ref, whole, gram, parts)
    basis_ref[...] = basis.T
    columns = []
    for k in range(4):
        held[k] = basis[:, 128 * k : 128 * k + 128]
        columns.append(jnp.concatenate([held[k, pl.ds(r, 32, stride=4), :] for r in range(4)], axis=0))
    basis = jnp.concatenate(columns, axis=1)
    basis_high, basis_low = split(basis)
    both = jnp.concatenate([basis_high, basis_low], axis=0)
    for copy in copies:
        copy.wait()
    for p in range(4):
        at = slice(512 * p, 512 * p + 512)
        twice = dot(both, high[:, at], NN)
        reduced = twice[:RANK] + twice[RANK:] + dot(basis_high, low[:, at], NN)
        reduced_ref[:, at] = reduced
        h, l = split(reduced.T)
        turned_high[:, 128 * p : 128 * p + 128] = h
        turned_low[:, 128 * p : 128 * p + 128] = l
    upper_gram(turned_high, turned_low, mine_out, other_out, whole, core_ref[0])


def second_basis_kernel(core_ref, mine_ref, other_ref, start_ref, reduced, basis_ref, core_out, whole, gram, parts, product):
    basis = leading(core_ref, mine_ref, other_ref, start_ref, whole, gram, parts)
    basis_ref[...] = basis.T
    basis = as_right_cols(basis)
    for p in range(4):
        product[128 * p : 128 * p + 128, :] = dot(as_left(reduced[:, 512 * p : 512 * p + 512]), basis, NT)
    row = lax.broadcasted_iota(jnp.int32, (8, 128), 0)
    group = lax.broadcasted_iota(jnp.int32, (8, 128), 1) // 16
    for q in range(32):
        for half in range(2):
            block = product[pl.ds(q + 256 * half, 8, stride=32), :]
            for bit in (1, 2, 4):
                up = pltpu.roll(pltpu.roll(block, 8 - bit, 0), 16 * bit, 1)
                down = pltpu.roll(pltpu.roll(block, bit, 0), 128 - 16 * bit, 1)
                same = (row & bit) == (group & bit)
                block = jnp.where(same, block, jnp.where((row & bit) == 0, up, down))
            core_out[pl.ds(16 * q + half, 8, stride=2), :] = block


def unpack_kernel(got_ref, out_ref):
    for half in range(2):
        for part in range(2):
            block = got_ref[pl.ds(256 * part + half, 128, stride=2), :].T
            for low in range(2):
                at = 256 * (2 * half + low) + 128 * part
                out_ref[:, :, at : at + 128] = block[64 * low : 64 * low + 64].reshape(4, 16, 128)


def shaped(*shape):
    return jax.ShapeDtypeStruct(shape, F32)


def shaped_half(*shape):
    return jax.ShapeDtypeStruct(shape, BF16)


LEADING_SCRATCH = [
    pltpu.VMEM((2, HALF, 8, 128), F32),
    pltpu.VMEM((N, N), F32),
    pltpu.VMEM((3 * N, N), BF16),
]


def in_vmem(x):
    return pltpu.with_memory_space_constraint(x, pltpu.VMEM)


def across_cores(x):
    return lax.ppermute(x, "c", [(0, 1), (1, 0)])


def total(mine, other):
    share = HALF // 16
    mine = (mine + across_cores(other)).reshape(16, share, 8, 128)
    got = jnp.sum(lax.all_to_all(mine, ("x", "y"), 0, 0, tiled=True), axis=0)
    got = jnp.sum(lax.all_to_all(jnp.broadcast_to(got, (8, share, 8, 128)), "z", 0, 0, tiled=True), axis=0)
    got = lax.all_to_all(jnp.broadcast_to(got, (16, share, 8, 128)), ("x", "y"), 0, 0, tiled=True)
    got = got.reshape(HALF, 8, 128)
    return in_vmem(got), in_vmem(across_cores(got))


def local(field, seeds_first, seeds_second):
    core = lax.axis_index("c").reshape(1)
    sent = pl.pallas_call(
        pack_kernel,
        out_shape=shaped(2, 128, 4, 8, 128),
        in_specs=[ANY],
        out_specs=ANY,
        scratch_shapes=[
            pltpu.VMEM((2, 8, 64, 1024), F32),
            pltpu.VMEM((2, 128, 4, 8, 128), F32),
            pltpu.SemaphoreType.DMA((8,)),
            pltpu.SemaphoreType.DMA((2,)),
        ],
        compiler_params=PARAMS,
    )(field.reshape(2, 8, 64, 1024))
    fibers = lax.all_to_all(sent.reshape(256, 4, 8, 128), ("z", "x", "y", "c"), 0, 0, tiled=True)
    starts = pl.pallas_call(
        seeds_kernel,
        out_shape=(pltpu.VMEM((RANK, N), F32), pltpu.VMEM((RANK, N), F32)),
        in_specs=[SMEM, VMEM, VMEM],
        compiler_params=PARAMS,
    )(core, seeds_first.T, seeds_second.T)
    fibers, starts = lax.optimization_barrier((fibers, starts))

    halves = (pltpu.VMEM((HALF, 8, 128), F32), pltpu.VMEM((HALF, 8, 128), F32))
    mine, other, high, low = pl.pallas_call(
        first_gram_kernel,
        out_shape=halves + (shaped_half(N, 2048), shaped_half(N, 2048)),
        in_specs=[SMEM, ANY],
        out_specs=(VMEM, VMEM, ANY, ANY),
        scratch_shapes=[
            pltpu.VMEM((32, 8, 4, 8, 128), F32),
            pltpu.VMEM((N, 2048), BF16),
            pltpu.VMEM((N, 2048), BF16),
            pltpu.VMEM((2, HALF, 8, 128), F32),
            pltpu.SemaphoreType.DMA((4,)),
            pltpu.SemaphoreType.DMA((2,)),
        ],
        compiler_params=PARAMS,
    )(core, fibers.reshape(32, 8, 4, 8, 128))
    mine, other = total(mine, other)
    basis_first, reduced, mine, other = pl.pallas_call(
        first_basis_kernel,
        out_shape=(shaped(N, RANK), pltpu.VMEM((RANK, 2048), F32)) + halves,
        in_specs=[SMEM, VMEM, VMEM, VMEM, ANY, ANY],
        out_specs=(VMEM, VMEM, VMEM, VMEM),
        scratch_shapes=LEADING_SCRATCH
        + [
            pltpu.VMEM((4, RANK, 128), F32),
            pltpu.VMEM((N, 2048), BF16),
            pltpu.VMEM((N, 2048), BF16),
            pltpu.VMEM((N, 4 * RANK), BF16),
            pltpu.VMEM((N, 4 * RANK), BF16),
            pltpu.SemaphoreType.DMA((2,)),
        ],
        compiler_params=PARAMS,
    )(core, mine, other, in_vmem(starts[0]), high, low)
    mine, other = total(mine, other)
    basis_second, ranks = pl.pallas_call(
        second_basis_kernel,
        out_shape=(shaped(N, RANK), pltpu.VMEM((512, 128), F32)),
        in_specs=[SMEM, VMEM, VMEM, VMEM, VMEM],
        out_specs=(VMEM, VMEM),
        scratch_shapes=LEADING_SCRATCH
        + [pltpu.VMEM((4 * RANK, RANK), F32)],
        compiler_params=PARAMS,
    )(core, mine, other, in_vmem(starts[1]), in_vmem(reduced))
    ranks = lax.all_to_all(ranks.reshape(256, 2, 128), ("z", "x", "y", "c"), 0, 0, tiled=True)
    core_tensor = pl.pallas_call(unpack_kernel, out_shape=shaped(4, 16, 1024), compiler_params=PARAMS)(
        in_vmem(ranks.reshape(512, 128))
    )
    return (basis_first, basis_second, core_tensor)


def solution(mesh):
    fine = Mesh(mesh.devices.reshape(8, 4, 4, 2), ("z", "x", "y", "c"))
    return jax.shard_map(
        local,
        mesh=fine,
        in_specs=(P(("z", "x"), ("y", "c"), None), P(), P()),
        out_specs=(P(), P(), P(("z", "x"), ("y", "c"), None)),
        check_vma=False,
    )
```

```python
import jax
import jax.numpy as jnp
from jax import lax
from jax.experimental import pallas as pl
from jax.experimental.pallas import tpu as pltpu
from jax.sharding import Mesh, PartitionSpec as P

ITERS = 4
N = 512
RANK = 128
F32 = jnp.float32
BF16 = jnp.bfloat16
NN = (((1,), (0,)), ((), ()))
NT = (((1,), (1,)), ((), ()))
TILES = [(row, col) for row in range(64) for col in range(row // 16, 4)]
HALF = len(TILES) // 2
PARAMS = pltpu.CompilerParams(vmem_limit_bytes=56 * 2**20)
VMEM = pl.BlockSpec(memory_space=pltpu.VMEM)
SMEM = pl.BlockSpec(memory_space=pltpu.SMEM)
ANY = pl.BlockSpec(memory_space=pl.ANY)


def dot(left, right, dims):
    return lax.dot_general(left, right, dims, preferred_element_type=F32)


def split(x):
    high = x.astype(BF16)
    return high, (x - high.astype(F32)).astype(BF16)


def as_left(x):
    high, low = split(x)
    return jnp.concatenate([high, low, high], axis=1)


def as_right_rows(x):
    high, low = split(x)
    return jnp.concatenate([high, high, low], axis=0)


def as_right_cols(x):
    high, low = split(x)
    return jnp.concatenate([high, high, low], axis=1)


def inverse_factor(inner, one):
    sub = lax.broadcasted_iota(jnp.int32, (8, RANK), 0)
    lane = lax.broadcasted_iota(jnp.int32, (8, RANK), 1)
    spread = lambda row: jnp.broadcast_to(row, (8, RANK))
    rest = [inner[8 * i : 8 * i + 8, :] for i in range(RANK // 8)]
    out = []
    for last in (8, 16):
        factor = []
        ready = None
        for p in range(last - 8, last):
            rows = range(p, last)
            column = lambda i, at: [spread(rest[i][:, at + t : at + t + 1]) for t in range(8)]
            cols = {i: column(i, 8 * p) for i in rows[1:]}
            cols[p] = ready or [col * one for col in column(p, 8 * p)]
            coming = {}
            if p + 1 < last:
                coming = {p: [col * one for col in column(p, 8 * p + 8)], p + 1: column(p + 1, 8 * p + 8)}
            panel = (lane >= 8 * p) & (lane < 8 * p + 8)
            for i in rows:
                unit = jnp.where(lane == sub + 8 * p, 1.0, 0.0) if i == p else 0.0
                rest[i] = jnp.where(panel, unit, rest[i])
            done = jnp.zeros((8, RANK), F32)
            pivots = jnp.ones((8, RANK), F32)
            for t in range(8):
                pivot = spread(cols[p][t][t : t + 1, :])
                row = spread(rest[p][t : t + 1, :])
                done = jnp.where(sub == t, row, done)
                pivots = jnp.where(sub == t, pivot, pivots)
                inverse = 1.0 / pivot
                ahead = [spread(cols[p][u][t : t + 1, :]) for u in range(t + 1, 8)]
                further = [spread(col[t : t + 1, :]) for col in coming[p]] if coming else []
                for i in rows:
                    scaled = cols[i][t] * inverse
                    for k, u in enumerate(range(t + 1, 8)):
                        cols[i][u] = cols[i][u] - scaled * ahead[k]
                    if i in coming and (i > p or t < 7):
                        coming[i] = [col - scaled * more for col, more in zip(coming[i], further)]
                    if i > p or t < 7:
                        rest[i] = rest[i] - scaled * row
            ready = coming.get(p + 1)
            done = done * lax.rsqrt(pivots)
            out.append(jnp.where(lane < 8 * p + 8, done, 0.0))
            factor.append(jnp.where((lane < 8 * p + 8) | (lane >= 8 * last), done, 0.0))
        if last < 16:
            factor = jnp.concatenate(factor, axis=0)
            change = lax.dot_general(
                factor[:, 8 * last :],
                factor,
                (((0,), (0,)), ((), ())),
                precision=lax.Precision.HIGHEST,
                preferred_element_type=F32,
            )
            for k, i in enumerate(range(last, 16)):
                rest[i] = jnp.where(lane < 8 * last, 0.0, rest[i]) - change[8 * k : 8 * k + 8]
    return jnp.concatenate(out, axis=0)


def ones(core_ref):
    return jnp.full((8, RANK), jnp.minimum(core_ref[0] + 1, 1).astype(F32))


def orthonormal(turned, one):
    inner = dot(as_left(turned), as_right_cols(turned), NT)
    return dot(as_left(inverse_factor(inner, one)), as_right_rows(turned), NN)


def seeds_kernel(core_ref, first_ref, second_ref, first_out, second_out):
    one = ones(core_ref)
    first_out[...] = orthonormal(first_ref[...].astype(F32), one)
    second_out[...] = orthonormal(second_ref[...].astype(F32), one)


def upper_gram(high, low, mine_ref, other_ref, swap, core):
    for block in range(2):
        rows, cols = slice(0, 256 * block + 256), slice(256 * block, 256 * block + 256)
        gram = dot(high[rows, :], high[cols, :], NT)
        gram += dot(low[rows, :], high[cols, :], NT)
        gram += dot(high[rows, :], low[cols, :], NT)
        for at, (row, col) in enumerate(TILES):
            if col // 2 == block:
                r, c = 8 * row, 128 * (col % 2)
                half = lax.bitwise_xor(at // HALF, core)
                swap[half, at % HALF] = gram[r : r + 8, c : c + 128]
    mine_ref[...] = swap[0]
    other_ref[...] = swap[1]


def pack_kernel(field_hbm, out_hbm, field, out, sems, out_sems):
    copies = [pltpu.make_async_copy(field_hbm.at[:, i], field.at[:, i], sems.at[i]) for i in range(8)]
    for copy in copies:
        copy.start()
    saves = []
    for half in range(2):
        for i in range(8):
            if half == 0:
                copies[i].wait()
            for p in range(4):
                at = slice(256 * p + 128 * half, 256 * p + 128 * half + 128)
                out[half, :, p, i, :] = jnp.concatenate([field[0, i, :, at], field[1, i, :, at]], axis=0).T
        saves.append(pltpu.make_async_copy(out.at[half], out_hbm.at[half], out_sems.at[half]))
        saves[half].start()
    for save in saves:
        save.wait()


def first_gram_kernel(core_ref, fibers_hbm, mine_ref, other_ref, high_hbm, low_hbm, fibers, high, low, swap, sems, out_sems):
    quarters = [slice(8 * q, 8 * q + 8) for q in range(4)]
    copies = [pltpu.make_async_copy(fibers_hbm.at[at], fibers.at[at], sems.at[q]) for q, at in enumerate(quarters)]
    for copy in copies:
        copy.start()
    first_half = lax.broadcasted_iota(jnp.int32, (8, 8, 128), 2) < 64
    for q in range(4):
        copies[q].wait()
        for p in range(4):
            for pair in range(4):
                one, two = fibers[quarters[q], 2 * pair, p], fibers[quarters[q], 2 * pair + 1, p]
                upper = jnp.where(first_half, one, pltpu.roll(two, 64, 2))
                lower = jnp.where(first_half, pltpu.roll(one, 64, 2), two)
                h, l = split(jnp.stack([upper, lower], axis=1).reshape(128, 128))
                at = slice(512 * p + 128 * pair, 512 * p + 128 * pair + 128)
                high[128 * q : 128 * q + 128, at] = h
                low[128 * q : 128 * q + 128, at] = l
    saves = [
        pltpu.make_async_copy(high, high_hbm, out_sems.at[0]),
        pltpu.make_async_copy(low, low_hbm, out_sems.at[1]),
    ]
    for save in saves:
        save.start()
    upper_gram(high, low, mine_ref, other_ref, swap, core_ref[0])
    for save in saves:
        save.wait()


def leading(core_ref, mine_ref, other_ref, start_ref, whole, gram, parts):
    core = core_ref[0]
    one = ones(core_ref)
    whole[core] = mine_ref[...]
    whole[1 - core] = other_ref[...]
    for at, (row, col) in enumerate(TILES):
        gram[8 * row : 8 * row + 8, 128 * col : 128 * col + 128] = whole[at // HALF, at % HALF]
    for row in range(1, 4):
        for col in range(row):
            gram[128 * row : 128 * row + 128, 128 * col : 128 * col + 128] = gram[
                128 * col : 128 * col + 128, 128 * row : 128 * row + 128
            ].T
    parts[...] = as_right_rows(gram[...])

    def sweep(_, basis):
        return orthonormal(dot(as_left(basis), parts[...], NN), one)

    return lax.fori_loop(0, ITERS, sweep, start_ref[...])


def first_basis_kernel(
    core_ref, mine_ref, other_ref, start_ref, high_hbm, low_hbm,
    basis_ref, reduced_ref, mine_out, other_out,
    whole, gram, parts, held, high, low, turned_high, turned_low, sems,
):
    copies = [pltpu.make_async_copy(high_hbm, high, sems.at[0]), pltpu.make_async_copy(low_hbm, low, sems.at[1])]
    for copy in copies:
        copy.start()
    basis = leading(core_ref, mine_ref, other_ref, start_ref, whole, gram, parts)
    basis_ref[...] = basis.T
    columns = []
    for k in range(4):
        held[k] = basis[:, 128 * k : 128 * k + 128]
        columns.append(jnp.concatenate([held[k, pl.ds(r, 32, stride=4), :] for r in range(4)], axis=0))
    basis = jnp.concatenate(columns, axis=1)
    basis_high, basis_low = split(basis)
    both = jnp.concatenate([basis_high, basis_low], axis=0)
    for copy in copies:
        copy.wait()
    for p in range(4):
        at = slice(512 * p, 512 * p + 512)
        twice = dot(both, high[:, at], NN)
        reduced = twice[:RANK] + twice[RANK:] + dot(basis_high, low[:, at], NN)
        reduced_ref[:, at] = reduced
        h, l = split(reduced.T)
        turned_high[:, 128 * p : 128 * p + 128] = h
        turned_low[:, 128 * p : 128 * p + 128] = l
    upper_gram(turned_high, turned_low, mine_out, other_out, whole, core_ref[0])


def second_basis_kernel(core_ref, mine_ref, other_ref, start_ref, reduced, basis_ref, core_out, whole, gram, parts, product):
    basis = leading(core_ref, mine_ref, other_ref, start_ref, whole, gram, parts)
    basis_ref[...] = basis.T
    basis = as_right_cols(basis)
    for p in range(4):
        product[128 * p : 128 * p + 128, :] = dot(as_left(reduced[:, 512 * p : 512 * p + 512]), basis, NT)
    row = lax.broadcasted_iota(jnp.int32, (8, 128), 0)
    group = lax.broadcasted_iota(jnp.int32, (8, 128), 1) // 16
    for q in range(32):
        for half in range(2):
            block = product[pl.ds(q + 256 * half, 8, stride=32), :]
            for bit in (1, 2, 4):
                up = pltpu.roll(pltpu.roll(block, 8 - bit, 0), 16 * bit, 1)
                down = pltpu.roll(pltpu.roll(block, bit, 0), 128 - 16 * bit, 1)
                same = (row & bit) == (group & bit)
                block = jnp.where(same, block, jnp.where((row & bit) == 0, up, down))
            core_out[pl.ds(16 * q + half, 8, stride=2), :] = block


def unpack_kernel(got_ref, out_ref):
    for half in range(2):
        for part in range(2):
            block = got_ref[pl.ds(256 * part + half, 128, stride=2), :].T
            for low in range(2):
                at = 256 * (2 * half + low) + 128 * part
                out_ref[:, :, at : at + 128] = block[64 * low : 64 * low + 64].reshape(4, 16, 128)


def shaped(*shape):
    return jax.ShapeDtypeStruct(shape, F32)


def shaped_half(*shape):
    return jax.ShapeDtypeStruct(shape, BF16)


LEADING_SCRATCH = [
    pltpu.VMEM((2, HALF, 8, 128), F32),
    pltpu.VMEM((N, N), F32),
    pltpu.VMEM((3 * N, N), BF16),
]


def in_vmem(x):
    return pltpu.with_memory_space_constraint(x, pltpu.VMEM)


def across_cores(x):
    return lax.ppermute(x, "c", [(0, 1), (1, 0)])


def total(mine, other):
    share = HALF // 16
    mine = (mine + across_cores(other)).reshape(16, share, 8, 128)
    got = jnp.sum(lax.all_to_all(mine, ("x", "y"), 0, 0, tiled=True), axis=0)
    got = jnp.sum(lax.all_to_all(jnp.broadcast_to(got, (8, share, 8, 128)), "z", 0, 0, tiled=True), axis=0)
    got = lax.all_to_all(jnp.broadcast_to(got, (16, share, 8, 128)), ("x", "y"), 0, 0, tiled=True)
    got = got.reshape(HALF, 8, 128)
    return in_vmem(got), in_vmem(across_cores(got))


def local(field, seeds_first, seeds_second):
    core = lax.axis_index("c").reshape(1)
    sent = pl.pallas_call(
        pack_kernel,
        out_shape=shaped(2, 128, 4, 8, 128),
        in_specs=[ANY],
        out_specs=ANY,
        scratch_shapes=[
            pltpu.VMEM((2, 8, 64, 1024), F32),
            pltpu.VMEM((2, 128, 4, 8, 128), F32),
            pltpu.SemaphoreType.DMA((8,)),
            pltpu.SemaphoreType.DMA((2,)),
        ],
        compiler_params=PARAMS,
    )(field.reshape(2, 8, 64, 1024))
    fibers = lax.all_to_all(sent.reshape(256, 4, 8, 128), ("z", "x", "y", "c"), 0, 0, tiled=True)
    starts = pl.pallas_call(
        seeds_kernel,
        out_shape=(pltpu.VMEM((RANK, N), F32), pltpu.VMEM((RANK, N), F32)),
        in_specs=[SMEM, VMEM, VMEM],
        compiler_params=PARAMS,
    )(core, seeds_first.T, seeds_second.T)
    fibers, starts = lax.optimization_barrier((fibers, starts))

    halves = (pltpu.VMEM((HALF, 8, 128), F32), pltpu.VMEM((HALF, 8, 128), F32))
    mine, other, high, low = pl.pallas_call(
        first_gram_kernel,
        out_shape=halves + (shaped_half(N, 2048), shaped_half(N, 2048)),
        in_specs=[SMEM, ANY],
        out_specs=(VMEM, VMEM, ANY, ANY),
        scratch_shapes=[
            pltpu.VMEM((32, 8, 4, 8, 128), F32),
            pltpu.VMEM((N, 2048), BF16),
            pltpu.VMEM((N, 2048), BF16),
            pltpu.VMEM((2, HALF, 8, 128), F32),
            pltpu.SemaphoreType.DMA((4,)),
            pltpu.SemaphoreType.DMA((2,)),
        ],
        compiler_params=PARAMS,
    )(core, fibers.reshape(32, 8, 4, 8, 128))
    mine, other = total(mine, other)
    basis_first, reduced, mine, other = pl.pallas_call(
        first_basis_kernel,
        out_shape=(shaped(N, RANK), pltpu.VMEM((RANK, 2048), F32)) + halves,
        in_specs=[SMEM, VMEM, VMEM, VMEM, ANY, ANY],
        out_specs=(VMEM, VMEM, VMEM, VMEM),
        scratch_shapes=LEADING_SCRATCH
        + [
            pltpu.VMEM((4, RANK, 128), F32),
            pltpu.VMEM((N, 2048), BF16),
            pltpu.VMEM((N, 2048), BF16),
            pltpu.VMEM((N, 4 * RANK), BF16),
            pltpu.VMEM((N, 4 * RANK), BF16),
            pltpu.SemaphoreType.DMA((2,)),
        ],
        compiler_params=PARAMS,
    )(core, mine, other, in_vmem(starts[0]), high, low)
    mine, other = total(mine, other)
    basis_second, ranks = pl.pallas_call(
        second_basis_kernel,
        out_shape=(shaped(N, RANK), pltpu.VMEM((512, 128), F32)),
        in_specs=[SMEM, VMEM, VMEM, VMEM, VMEM],
        out_specs=(VMEM, VMEM),
        scratch_shapes=LEADING_SCRATCH
        + [pltpu.VMEM((4 * RANK, RANK), F32)],
        compiler_params=PARAMS,
    )(core, mine, other, in_vmem(starts[1]), in_vmem(reduced))
    ranks = lax.all_to_all(ranks.reshape(256, 2, 128), ("z", "x", "y", "c"), 0, 0, tiled=True)
    core_tensor = pl.pallas_call(unpack_kernel, out_shape=shaped(4, 16, 1024), compiler_params=PARAMS)(
        in_vmem(ranks.reshape(512, 128))
    )
    return (basis_first, basis_second, core_tensor)


def solution(mesh):
    fine = Mesh(mesh.devices.reshape(8, 4, 4, 2), ("z", "x", "y", "c"))
    return jax.shard_map(
        local,
        mesh=fine,
        in_specs=(P(("z", "x"), ("y", "c"), None), P(), P()),
        out_specs=(P(), P(), P(("z", "x"), ("y", "c"), None)),
        check_vma=False,
    )
```

```python
import jax
import jax.numpy as jnp
from jax import lax
from jax.experimental import pallas as pl
from jax.experimental.pallas import tpu as pltpu
from jax.sharding import Mesh, PartitionSpec as P

ITERS = 4
N = 512
RANK = 128
F32 = jnp.float32
BF16 = jnp.bfloat16
NN = (((1,), (0,)), ((), ()))
NT = (((1,), (1,)), ((), ()))
TILES = [(row, col) for row in range(64) for col in range(row // 16, 4)]
HALF = len(TILES) // 2
PARAMS = pltpu.CompilerParams(vmem_limit_bytes=56 * 2**20)
VMEM = pl.BlockSpec(memory_space=pltpu.VMEM)
SMEM = pl.BlockSpec(memory_space=pltpu.SMEM)
ANY = pl.BlockSpec(memory_space=pl.ANY)


def dot(left, right, dims):
    return lax.dot_general(left, right, dims, preferred_element_type=F32)


def split(x):
    high = x.astype(BF16)
    return high, (x - high.astype(F32)).astype(BF16)


def as_left(x):
    high, low = split(x)
    return jnp.concatenate([high, low, high], axis=1)


def as_right_rows(x):
    high, low = split(x)
    return jnp.concatenate([high, high, low], axis=0)


def as_right_cols(x):
    high, low = split(x)
    return jnp.concatenate([high, high, low], axis=1)


def inverse_factor(inner, one):
    sub = lax.broadcasted_iota(jnp.int32, (8, RANK), 0)
    lane = lax.broadcasted_iota(jnp.int32, (8, RANK), 1)
    spread = lambda row: jnp.broadcast_to(row, (8, RANK))
    rest = [inner[8 * i : 8 * i + 8, :] for i in range(RANK // 8)]
    out = []
    for last in (8, 16):
        factor = []
        ready = None
        for p in range(last - 8, last):
            rows = range(p, last)
            column = lambda i, at: [spread(rest[i][:, at + t : at + t + 1]) for t in range(8)]
            cols = {i: column(i, 8 * p) for i in rows[1:]}
            cols[p] = ready or [col * one for col in column(p, 8 * p)]
            coming = {}
            if p + 1 < last:
                coming = {p: [col * one for col in column(p, 8 * p + 8)], p + 1: column(p + 1, 8 * p + 8)}
            panel = (lane >= 8 * p) & (lane < 8 * p + 8)
            for i in rows:
                unit = jnp.where(lane == sub + 8 * p, 1.0, 0.0) if i == p else 0.0
                rest[i] = jnp.where(panel, unit, rest[i])
            done = jnp.zeros((8, RANK), F32)
            pivots = jnp.ones((8, RANK), F32)
            for t in range(8):
                pivot = spread(cols[p][t][t : t + 1, :])
                row = spread(rest[p][t : t + 1, :])
                done = jnp.where(sub == t, row, done)
                pivots = jnp.where(sub == t, pivot, pivots)
                inverse = 1.0 / pivot
                ahead = [spread(cols[p][u][t : t + 1, :]) for u in range(t + 1, 8)]
                further = [spread(col[t : t + 1, :]) for col in coming[p]] if coming else []
                for i in rows:
                    scaled = cols[i][t] * inverse
                    for k, u in enumerate(range(t + 1, 8)):
                        cols[i][u] = cols[i][u] - scaled * ahead[k]
                    if i in coming and (i > p or t < 7):
                        coming[i] = [col - scaled * more for col, more in zip(coming[i], further)]
                    if i > p or t < 7:
                        rest[i] = rest[i] - scaled * row
            ready = coming.get(p + 1)
            done = done * lax.rsqrt(pivots)
            out.append(jnp.where(lane < 8 * p + 8, done, 0.0))
            factor.append(jnp.where((lane < 8 * p + 8) | (lane >= 8 * last), done, 0.0))
        if last < 16:
            factor = jnp.concatenate(factor, axis=0)
            high, low = split(factor)
            change = dot(
                jnp.concatenate([high, low, high], axis=0)[:, 8 * last :],
                jnp.concatenate([high, high, low], axis=0),
                (((0,), (0,)), ((), ())),
            )
            for k, i in enumerate(range(last, 16)):
                rest[i] = jnp.where(lane < 8 * last, 0.0, rest[i]) - change[8 * k : 8 * k + 8]
    return jnp.concatenate(out, axis=0)


def ones(core_ref):
    return jnp.full((8, RANK), jnp.minimum(core_ref[0] + 1, 1).astype(F32))


def orthonormal(turned, one):
    inner = dot(as_left(turned), as_right_cols(turned), NT)
    return dot(as_left(inverse_factor(inner, one)), as_right_rows(turned), NN)


def seeds_kernel(core_ref, first_ref, second_ref, first_out, second_out):
    one = ones(core_ref)
    first_out[...] = orthonormal(first_ref[...].astype(F32), one)
    second_out[...] = orthonormal(second_ref[...].astype(F32), one)


def upper_gram(high, low, mine_ref, other_ref, swap, core):
    for block in range(2):
        rows, cols = slice(0, 256 * block + 256), slice(256 * block, 256 * block + 256)
        gram = dot(high[rows, :], high[cols, :], NT)
        gram += dot(low[rows, :], high[cols, :], NT)
        gram += dot(high[rows, :], low[cols, :], NT)
        for at, (row, col) in enumerate(TILES):
            if col // 2 == block:
                r, c = 8 * row, 128 * (col % 2)
                half = lax.bitwise_xor(at // HALF, core)
                swap[half, at % HALF] = gram[r : r + 8, c : c + 128]
    mine_ref[...] = swap[0]
    other_ref[...] = swap[1]


def pack_kernel(field_hbm, out_hbm, field, out, sems, out_sems):
    copies = [pltpu.make_async_copy(field_hbm.at[:, i], field.at[:, i], sems.at[i]) for i in range(8)]
    for copy in copies:
        copy.start()
    saves = []
    for half in range(2):
        for i in range(8):
            if half == 0:
                copies[i].wait()
            for p in range(4):
                at = slice(256 * p + 128 * half, 256 * p + 128 * half + 128)
                out[half, :, p, i, :] = jnp.concatenate([field[0, i, :, at], field[1, i, :, at]], axis=0).T
        saves.append(pltpu.make_async_copy(out.at[half], out_hbm.at[half], out_sems.at[half]))
        saves[half].start()
    for save in saves:
        save.wait()


def first_gram_kernel(core_ref, fibers_hbm, mine_ref, other_ref, high_hbm, low_hbm, fibers, high, low, swap, sems, out_sems):
    quarters = [slice(8 * q, 8 * q + 8) for q in range(4)]
    copies = [pltpu.make_async_copy(fibers_hbm.at[at], fibers.at[at], sems.at[q]) for q, at in enumerate(quarters)]
    for copy in copies:
        copy.start()
    first_half = lax.broadcasted_iota(jnp.int32, (8, 8, 128), 2) < 64
    for q in range(4):
        copies[q].wait()
        for p in range(4):
            for pair in range(4):
                one, two = fibers[quarters[q], 2 * pair, p], fibers[quarters[q], 2 * pair + 1, p]
                upper = jnp.where(first_half, one, pltpu.roll(two, 64, 2))
                lower = jnp.where(first_half, pltpu.roll(one, 64, 2), two)
                h, l = split(jnp.stack([upper, lower], axis=1).reshape(128, 128))
                at = slice(512 * p + 128 * pair, 512 * p + 128 * pair + 128)
                high[128 * q : 128 * q + 128, at] = h
                low[128 * q : 128 * q + 128, at] = l
    saves = [
        pltpu.make_async_copy(high, high_hbm, out_sems.at[0]),
        pltpu.make_async_copy(low, low_hbm, out_sems.at[1]),
    ]
    for save in saves:
        save.start()
    upper_gram(high, low, mine_ref, other_ref, swap, core_ref[0])
    for save in saves:
        save.wait()


def leading(core_ref, mine_ref, other_ref, start_ref, whole, gram, parts):
    core = core_ref[0]
    one = ones(core_ref)
    whole[core] = mine_ref[...]
    whole[1 - core] = other_ref[...]
    for at, (row, col) in enumerate(TILES):
        gram[8 * row : 8 * row + 8, 128 * col : 128 * col + 128] = whole[at // HALF, at % HALF]
    for row in range(1, 4):
        for col in range(row):
            gram[128 * row : 128 * row + 128, 128 * col : 128 * col + 128] = gram[
                128 * col : 128 * col + 128, 128 * row : 128 * row + 128
            ].T
    parts[...] = as_right_rows(gram[...])

    def sweep(_, basis):
        return orthonormal(dot(as_left(basis), parts[...], NN), one)

    return lax.fori_loop(0, ITERS, sweep, start_ref[...])


def first_basis_kernel(
    core_ref, mine_ref, other_ref, start_ref, high_hbm, low_hbm,
    basis_ref, reduced_ref, mine_out, other_out,
    whole, gram, parts, held, high, low, turned_high, turned_low, sems,
):
    copies = [pltpu.make_async_copy(high_hbm, high, sems.at[0]), pltpu.make_async_copy(low_hbm, low, sems.at[1])]
    for copy in copies:
        copy.start()
    basis = leading(core_ref, mine_ref, other_ref, start_ref, whole, gram, parts)
    basis_ref[...] = basis.T
    columns = []
    for k in range(4):
        held[k] = basis[:, 128 * k : 128 * k + 128]
        columns.append(jnp.concatenate([held[k, pl.ds(r, 32, stride=4), :] for r in range(4)], axis=0))
    basis = jnp.concatenate(columns, axis=1)
    basis_high, basis_low = split(basis)
    both = jnp.concatenate([basis_high, basis_low], axis=0)
    for copy in copies:
        copy.wait()
    for p in range(4):
        at = slice(512 * p, 512 * p + 512)
        twice = dot(both, high[:, at], NN)
        reduced = twice[:RANK] + twice[RANK:] + dot(basis_high, low[:, at], NN)
        reduced_ref[:, at] = reduced
        h, l = split(reduced.T)
        turned_high[:, 128 * p : 128 * p + 128] = h
        turned_low[:, 128 * p : 128 * p + 128] = l
    upper_gram(turned_high, turned_low, mine_out, other_out, whole, core_ref[0])


def second_basis_kernel(core_ref, mine_ref, other_ref, start_ref, reduced, basis_ref, core_out, whole, gram, parts, product):
    basis = leading(core_ref, mine_ref, other_ref, start_ref, whole, gram, parts)
    basis_ref[...] = basis.T
    basis = as_right_cols(basis)
    for p in range(4):
        product[128 * p : 128 * p + 128, :] = dot(as_left(reduced[:, 512 * p : 512 * p + 512]), basis, NT)
    row = lax.broadcasted_iota(jnp.int32, (8, 128), 0)
    group = lax.broadcasted_iota(jnp.int32, (8, 128), 1) // 16
    for q in range(32):
        for half in range(2):
            block = product[pl.ds(q + 256 * half, 8, stride=32), :]
            for bit in (1, 2, 4):
                up = pltpu.roll(pltpu.roll(block, 8 - bit, 0), 16 * bit, 1)
                down = pltpu.roll(pltpu.roll(block, bit, 0), 128 - 16 * bit, 1)
                same = (row & bit) == (group & bit)
                block = jnp.where(same, block, jnp.where((row & bit) == 0, up, down))
            core_out[pl.ds(16 * q + half, 8, stride=2), :] = block


def unpack_kernel(got_ref, out_ref):
    for half in range(2):
        for part in range(2):
            block = got_ref[pl.ds(256 * part + half, 128, stride=2), :].T
            for low in range(2):
                at = 256 * (2 * half + low) + 128 * part
                out_ref[:, :, at : at + 128] = block[64 * low : 64 * low + 64].reshape(4, 16, 128)


def shaped(*shape):
    return jax.ShapeDtypeStruct(shape, F32)


def shaped_half(*shape):
    return jax.ShapeDtypeStruct(shape, BF16)


LEADING_SCRATCH = [
    pltpu.VMEM((2, HALF, 8, 128), F32),
    pltpu.VMEM((N, N), F32),
    pltpu.VMEM((3 * N, N), BF16),
]


def in_vmem(x):
    return pltpu.with_memory_space_constraint(x, pltpu.VMEM)


def across_cores(x):
    return lax.ppermute(x, "c", [(0, 1), (1, 0)])


def total(mine, other):
    share = HALF // 16
    mine = (mine + across_cores(other)).reshape(16, share, 8, 128)
    got = jnp.sum(lax.all_to_all(mine, ("x", "y"), 0, 0, tiled=True), axis=0)
    got = jnp.sum(lax.all_to_all(jnp.broadcast_to(got, (8, share, 8, 128)), "z", 0, 0, tiled=True), axis=0)
    got = lax.all_to_all(jnp.broadcast_to(got, (16, share, 8, 128)), ("x", "y"), 0, 0, tiled=True)
    got = got.reshape(HALF, 8, 128)
    return in_vmem(got), in_vmem(across_cores(got))


def local(field, seeds_first, seeds_second):
    core = lax.axis_index("c").reshape(1)
    sent = pl.pallas_call(
        pack_kernel,
        out_shape=shaped(2, 128, 4, 8, 128),
        in_specs=[ANY],
        out_specs=ANY,
        scratch_shapes=[
            pltpu.VMEM((2, 8, 64, 1024), F32),
            pltpu.VMEM((2, 128, 4, 8, 128), F32),
            pltpu.SemaphoreType.DMA((8,)),
            pltpu.SemaphoreType.DMA((2,)),
        ],
        compiler_params=PARAMS,
    )(field.reshape(2, 8, 64, 1024))
    fibers = lax.all_to_all(sent.reshape(256, 4, 8, 128), ("z", "x", "y", "c"), 0, 0, tiled=True)
    starts = pl.pallas_call(
        seeds_kernel,
        out_shape=(pltpu.VMEM((RANK, N), F32), pltpu.VMEM((RANK, N), F32)),
        in_specs=[SMEM, VMEM, VMEM],
        compiler_params=PARAMS,
    )(core, seeds_first.T, seeds_second.T)
    fibers, starts = lax.optimization_barrier((fibers, starts))

    halves = (pltpu.VMEM((HALF, 8, 128), F32), pltpu.VMEM((HALF, 8, 128), F32))
    mine, other, high, low = pl.pallas_call(
        first_gram_kernel,
        out_shape=halves + (shaped_half(N, 2048), shaped_half(N, 2048)),
        in_specs=[SMEM, ANY],
        out_specs=(VMEM, VMEM, ANY, ANY),
        scratch_shapes=[
            pltpu.VMEM((32, 8, 4, 8, 128), F32),
            pltpu.VMEM((N, 2048), BF16),
            pltpu.VMEM((N, 2048), BF16),
            pltpu.VMEM((2, HALF, 8, 128), F32),
            pltpu.SemaphoreType.DMA((4,)),
            pltpu.SemaphoreType.DMA((2,)),
        ],
        compiler_params=PARAMS,
    )(core, fibers.reshape(32, 8, 4, 8, 128))
    mine, other = total(mine, other)
    basis_first, reduced, mine, other = pl.pallas_call(
        first_basis_kernel,
        out_shape=(shaped(N, RANK), pltpu.VMEM((RANK, 2048), F32)) + halves,
        in_specs=[SMEM, VMEM, VMEM, VMEM, ANY, ANY],
        out_specs=(VMEM, VMEM, VMEM, VMEM),
        scratch_shapes=LEADING_SCRATCH
        + [
            pltpu.VMEM((4, RANK, 128), F32),
            pltpu.VMEM((N, 2048), BF16),
            pltpu.VMEM((N, 2048), BF16),
            pltpu.VMEM((N, 4 * RANK), BF16),
            pltpu.VMEM((N, 4 * RANK), BF16),
            pltpu.SemaphoreType.DMA((2,)),
        ],
        compiler_params=PARAMS,
    )(core, mine, other, in_vmem(starts[0]), high, low)
    mine, other = total(mine, other)
    basis_second, ranks = pl.pallas_call(
        second_basis_kernel,
        out_shape=(shaped(N, RANK), pltpu.VMEM((512, 128), F32)),
        in_specs=[SMEM, VMEM, VMEM, VMEM, VMEM],
        out_specs=(VMEM, VMEM),
        scratch_shapes=LEADING_SCRATCH
        + [pltpu.VMEM((4 * RANK, RANK), F32)],
        compiler_params=PARAMS,
    )(core, mine, other, in_vmem(starts[1]), in_vmem(reduced))
    ranks = lax.all_to_all(ranks.reshape(256, 2, 128), ("z", "x", "y", "c"), 0, 0, tiled=True)
    core_tensor = pl.pallas_call(unpack_kernel, out_shape=shaped(4, 16, 1024), compiler_params=PARAMS)(
        in_vmem(ranks.reshape(512, 128))
    )
    return (basis_first, basis_second, core_tensor)


def solution(mesh):
    fine = Mesh(mesh.devices.reshape(8, 4, 4, 2), ("z", "x", "y", "c"))
    return jax.shard_map(
        local,
        mesh=fine,
        in_specs=(P(("z", "x"), ("y", "c"), None), P(), P()),
        out_specs=(P(), P(), P(("z", "x"), ("y", "c"), None)),
        check_vma=False,
    )
```
